32 devices in a mesh: ctx: 2 (over x), tok: 8 (over z, core), head: 2 (over y).
Axes of the slice: x: 2, y: 2, z: 4, core: 2. Of those that a mesh axis runs over, the one named last changes fastest.
Arguments:
- keys: bfloat16 [2, 2, 4, 6144, 256], P(None, 'ctx', 'head', 'tok'), may hold values from -6 to 6
- values: bfloat16 [2, 2, 4, 6144, 256], P(None, 'ctx', 'head', 'tok'), may hold values from -6 to 6
- queries: bfloat16 [2, 2, 4, 6144, 256], P(None, 'ctx', 'head', 'tok'), may hold values from -6 to 6
- rates: float32 [2, 2, 4, 6144], P(None, 'ctx', 'head', 'tok'), may hold values from 0.1 to 3, as said below
- state_in: bfloat16 [2, 4, 3, 256, 512], P('ctx', 'head'), may hold values from -0.375 to 0.375
- fresh: bfloat16 [4, 3, 256, 512], P('head'), may hold values from -0.375 to 0.375
Outputs:
- outputs: bfloat16 [2, 2, 4, 6144, 256], P(None, 'ctx', 'head', 'tok')
The draws below stay inside these ranges and needn't reach their ends.
Inputs may be any that keep to these rules, and one draw needn't show every extreme that they name: Positive per-token learning rates.
All inputs are finite; a program needn't handle non-finite values.
Results may differ from the reference program's by a relative error of at most 0.023.
Values may be sent and summed in bfloat16 or wider, within the bound.
No kernel may reach another device: no remote copies, remote signals or barrier semaphores. Data moves between devices by JAX's collectives and lax.ppermute only.
A program may use at most 64 MiB of HBM per device.

```python
import jax
import jax.numpy as jnp
from jax import lax

DH = 256
DF = 512
TOK_DEV = 768
HEADS = 4
SPAN = 6144
SPANS = 2
N_TOK = 8


def draw_rates(key, part):
    shape = (2, SPANS, HEADS, SPAN)
    base = jnp.exp(jax.random.uniform(key, shape, jnp.float32, jnp.log(0.1), 0.0))
    rise = 3.0 ** (jnp.arange(HEADS, dtype=jnp.float32) / max(HEADS - 1, 1))
    return base * rise[None, None, :, None]


def block_scale(key, dims, cuts, smallest, top_value):
    def one(dim, blocks):
        draws = jax.random.uniform(jax.random.fold_in(jax.random.fold_in(key, 6), dim), (blocks,), jnp.float32, smallest / len(cuts), top_value / len(cuts))
        return jnp.repeat(jnp.exp(draws), dims[dim] // blocks).reshape((-1,) + (1,) * (len(dims) - dim - 1))

    factor_of = one(*cuts[0])
    for cut in cuts[1:]:
        factor_of = factor_of * one(*cut)
    return factor_of


def gaussian(key, shape, scale, bound, pieces=(), kind=jnp.bfloat16):
    array = jax.random.normal(key, shape, jnp.float32) * scale
    if len(pieces) > 0:
        array = block_scale(key, shape, pieces, -0.22, 0.18) * array
    return jnp.clip(array, min=-bound, max=bound).astype(kind)


def setup_inputs(seed: int = 0) -> dict:
    splits = jax.random.split(jax.random.key(seed), 7)
    keys = gaussian(splits[0], (2, SPANS, HEADS, SPAN, DH), 1.0, 6.0, ((1, 2), (2, 2), (3, 8)))
    values = gaussian(splits[1], (2, SPANS, HEADS, SPAN, DH), 1.0, 6.0, ((1, 2), (2, 2), (3, 8)))
    queries = gaussian(splits[2], (2, SPANS, HEADS, SPAN, DH), 1.0, 6.0, ((1, 2), (2, 2), (3, 8)))
    rates = draw_rates(jax.random.fold_in(splits[6], 71), 0)
    state_in = gaussian(splits[4], (SPANS, HEADS, 3, DH, DF), DH ** -0.5, 0.375, ((0, 2), (1, 2)))
    fresh = gaussian(splits[5], (HEADS, 3, DH, DF), DH ** -0.5, 0.375, ((0, 2),))
    return {"keys": keys, "values": values, "queries": queries, "rates": rates, "state_in": state_in, "fresh": fresh}


def partial_grads(state, keys_p, values_p, rate_p):
    w_one = state[0]
    w_three = state[1]
    w_back = state[2]
    h_one = jnp.dot(keys_p, w_one, preferred_element_type=jnp.float32)
    h_three = jnp.dot(keys_p, w_three, preferred_element_type=jnp.float32)
    sig = jax.nn.sigmoid(h_one)
    act = (h_one * sig * h_three).astype(jnp.bfloat16)
    weighted = (rate_p[:, None] * values_p.astype(jnp.float32)).astype(jnp.bfloat16)
    dact = -jnp.dot(weighted, w_back, preferred_element_type=jnp.float32)
    d_one = (dact * h_three * sig * (1.0 + h_one * (1.0 - sig))).astype(jnp.bfloat16)
    d_three = (dact * h_one * sig).astype(jnp.bfloat16)
    g_one = jnp.dot(keys_p.T, d_one, preferred_element_type=jnp.float32)
    g_three = jnp.dot(keys_p.T, d_three, preferred_element_type=jnp.float32)
    g_back = -jnp.dot(weighted.T, act, preferred_element_type=jnp.float32)
    return jnp.stack([g_one, g_three, g_back])

def head_grads(state, keys_h, values_h, rates_h):
    total = jnp.zeros(state.shape, jnp.float32)
    for piece in range(N_TOK):
        lo = piece * TOK_DEV
        part_grad = partial_grads(state, keys_h[lo:lo + TOK_DEV], values_h[lo:lo + TOK_DEV], rates_h[lo:lo + TOK_DEV])
        part_grad = lax.optimization_barrier(part_grad.astype(jnp.bfloat16))
        total = total + part_grad.astype(jnp.float32)
    return total

def apply_state(state, queries_h):
    p_one = jnp.dot(queries_h, state[0], preferred_element_type=jnp.float32)
    p_three = jnp.dot(queries_h, state[1], preferred_element_type=jnp.float32)
    mixed = (jax.nn.silu(p_one) * p_three).astype(jnp.bfloat16)
    return jnp.dot(mixed, state[2].T, preferred_element_type=jnp.float32).astype(jnp.bfloat16)

def update_block(states, keys_c, values_c, rates_c):
    grads = jax.vmap(head_grads)(states, keys_c, values_c, rates_c)
    total_sq = jnp.sum(grads * grads)
    scale = 0.5 * jnp.sqrt(jnp.float32(3 * DF * HEADS)) / jnp.sqrt(total_sq + 1e-06)
    older = states.astype(jnp.float32)
    moved = older - scale * grads
    old_norm = jnp.sqrt(lax.optimization_barrier(jnp.sum(older * older, axis=-2, keepdims=True)))
    new_norm = jnp.sqrt(lax.optimization_barrier(jnp.sum(moved * moved, axis=-2, keepdims=True)) + 1e-06)
    return (moved * old_norm / new_norm).astype(jnp.bfloat16)

def reference(keys, values, queries, rates, state_in, fresh):
    first_states = []
    first_outs = []
    for block in range(SPANS):
        newer = update_block(state_in[block], keys[0, block], values[0, block], rates[0, block])
        first_states.append(newer)
        first_outs.append(jax.vmap(apply_state)(newer, queries[0, block]))
    second_outs = []
    for block in range(SPANS):
        incoming = fresh if block == 0 else first_states[block - 1]
        newer = update_block(incoming, keys[1, block], values[1, block], rates[1, block])
        second_outs.append(jax.vmap(apply_state)(newer, queries[1, block]))
    return jnp.stack([jnp.stack(first_outs), jnp.stack(second_outs)])
```

```python
import functools

import jax
import jax.numpy as jnp
from jax import lax
from jax.experimental import pallas as pl
from jax.experimental.pallas import tpu as pltpu
from jax.sharding import PartitionSpec as P

BF16 = jnp.bfloat16
F32 = jnp.float32
VMEM = pl.BlockSpec(memory_space=pltpu.VMEM)
SMEM = pl.BlockSpec(memory_space=pltpu.SMEM)


def matmul(a, b, contract=((1,), (0,))):
    return lax.dot_general(a, b, (contract, ((), ())), preferred_element_type=F32)


def sigmoid(x):
    return 0.5 * jnp.tanh(0.5 * x) + 0.5


def add_grads(state, pairs, acc, wide):
    hidden = state.shape[2]
    for index, (keys, weighted) in enumerate(pairs):
        for lo in range(0, hidden, wide):
            cols = slice(lo, lo + wide)
            h_one = matmul(keys, state[0, :, cols])
            h_three = matmul(keys, state[1, :, cols])
            dact = matmul(weighted, state[2, :, cols])
            sig = sigmoid(h_one)
            gated = h_one * sig
            act = (gated * h_three).astype(BF16)
            d_three = (dact * gated).astype(BF16)
            d_one = (dact * h_three * (sig + gated - gated * sig)).astype(BF16)
            for m, (left, right) in enumerate(((keys, d_one), (keys, d_three), (weighted, act))):
                part = matmul(left, right, ((0,), (0,)))
                if index == 0:
                    acc[m, :, cols] = part
                else:
                    acc[m, :, cols] += part


def put_shards(acc, row, outs):
    rows = outs[0].shape[1]
    for d, out in enumerate(outs):
        start = pl.multiple_of((row ^ d) * rows, rows)
        for m in range(acc.shape[0]):
            out[m] = acc[m, pl.ds(start, rows), :].astype(BF16)


def renorm(older, shards, row, total_sq, factor, moved, newer):
    rows = shards[0].shape[1]
    scale = factor * lax.rsqrt(total_sq[0:1, 0:1] + 1e-06)
    for m in range(older.shape[0]):
        old_sq = 0.0
        new_sq = 0.0
        for d, shard in enumerate(shards):
            start = pl.multiple_of((row ^ d) * rows, rows)
            old = older[m, pl.ds(start, rows), :].astype(F32)
            new = old + scale * shard[m].astype(F32)
            moved[pl.ds(start, rows), :] = new
            old_sq = old_sq + jnp.sum(old * old, axis=0, keepdims=True)
            new_sq = new_sq + jnp.sum(new * new, axis=0, keepdims=True)
        ratio = jnp.sqrt(old_sq) * lax.rsqrt(new_sq + 1e-06)
        newer[m] = (moved[...] * ratio).astype(BF16)


def applied(state, queries):
    p_one = matmul(queries, state[0])
    p_three = matmul(queries, state[1])
    mixed = (p_one * sigmoid(p_one) * p_three).astype(BF16)
    return matmul(mixed, state[2], ((1,), (1,))).astype(BF16)


def call(body, name, outs, specs, scratch, *args):
    return pl.pallas_call(
        body,
        out_shape=outs,
        in_specs=specs,
        out_specs=jax.tree.map(lambda _: VMEM, outs),
        scratch_shapes=scratch,
        name=name,
    )(*args)


def shape(*dims, dtype=BF16):
    return jax.ShapeDtypeStruct(dims, dtype)


def first_grads(where, state, mine, others, weighted, weighted_others):
    _, dims, hidden = state.shape
    count = lax.axis_size("tok") // 2
    outs = [shape(3, dims // count, hidden) for _ in range(count)]

    def body(where, state, mine, weighted, others, weighted_others, *rest):
        outs, acc = rest[:count], rest[count]
        pairs = [(mine[...], weighted[...]), (others[...], weighted_others[...])]
        add_grads(state, pairs, acc, 256)
        put_shards(acc, where[0], outs)

    return call(
        body, "first_grads", outs, [SMEM] + [VMEM] * 5, [pltpu.VMEM((3, dims, hidden), F32)],
        where, state, mine, weighted, others, weighted_others,
    )


def next_grads(where, older, shards, total_sq, factor, fresh, mine, others, weighted, weighted_others):
    _, dims, hidden = older.shape
    count = len(shards)
    outs = [shape(3, dims, hidden)] + [shape(3, dims // count, hidden) for _ in range(count)]

    def body(where, older, total_sq, fresh, mine, weighted, others, weighted_others, *rest):
        shards, newer, outs = rest[:count], rest[count], rest[count + 1 : 2 * count + 1]
        moved, state, acc = rest[2 * count + 1 :]
        renorm(older, shards, where[0], total_sq, factor, moved, newer)

        @pl.when(where[1] == 0)
        def _():
            state[...] = fresh[...]

        @pl.when(where[1] != 0)
        def _():
            state[...] = newer[...]

        pairs = [(mine[...], weighted[...]), (others[...], weighted_others[...])]
        add_grads(state, pairs, acc, 256)
        put_shards(acc, where[0], outs)

    scratch = [
        pltpu.VMEM((dims, hidden), F32), pltpu.VMEM((3, dims, hidden), BF16), pltpu.VMEM((3, dims, hidden), F32),
    ]
    got = call(
        body, "next_grads", outs, [SMEM] + [VMEM] * (7 + count), scratch,
        where, older, total_sq, fresh, mine, weighted, others, weighted_others, *shards,
    )
    return got[0], got[1:]


def shard_sum(parts):
    def body(*refs):
        parts, (out, square) = refs[:-2], refs[-2:]
        total_sq = 0.0
        for m in range(out.shape[0]):
            total = parts[0][m].astype(F32)
            for part in parts[1:]:
                total = total + part[m].astype(F32)
            out[m] = total.astype(BF16)
            total_sq = total_sq + jnp.sum(total * total, axis=(0, 1), keepdims=True)
        square[...] = jnp.broadcast_to(total_sq, square.shape)

    outs = [shape(*parts[0].shape), shape(8, 128, dtype=F32)]
    return call(body, "shard_sum", outs, [VMEM] * len(parts), [], *parts)


def apply_old(state, mine, others):
    def body(state, mine, others, out, out_others):
        out_others[...] = applied(state, others[...])
        out[...] = applied(state, mine[...])

    outs = [shape(*mine.shape), shape(*mine.shape)]
    return call(body, "apply_old", outs, [VMEM] * 3, [], state, mine, others)


def apply_new(where, older, shards, total_sq, factor, mine, others):
    _, dims, hidden = older.shape
    count = len(shards)

    def body(where, older, total_sq, mine, others, *rest):
        shards, out, out_others, moved, newer = rest[:count], *rest[count:]
        renorm(older, shards, where[0], total_sq, factor, moved, newer)
        out_others[...] = applied(newer, others[...])
        out[...] = applied(newer, mine[...])

    outs = [shape(*mine.shape), shape(*mine.shape)]
    scratch = [pltpu.VMEM((dims, hidden), F32), pltpu.VMEM((3, dims, hidden), BF16)]
    return call(
        body, "apply_new", outs, [SMEM] + [VMEM] * (4 + count), scratch,
        where, older, total_sq, mine, others, *shards,
    )


def after(value, *others):
    return lax.optimization_barrier((value, *others))[0]


def total_over(square, axis, step):
    while step < lax.axis_size(axis):
        pairs = [(i, i ^ step) for i in range(lax.axis_size(axis))]
        square = square + lax.ppermute(square, axis, pairs)
        step *= 2
    return square


def shards(keys, values, queries, rates, state_in, fresh):
    blocks, tok = lax.axis_size("ctx"), lax.axis_size("tok")
    heads_all = lax.axis_size("head") * state_in.shape[1]
    hidden = state_in.shape[-1]
    count = tok // 2
    assert state_in.shape[1] == 2 and tok == 2 * count and count & (count - 1) == 0
    factor = 0.5 * float(3 * hidden * heads_all) ** 0.5
    core = lax.axis_index("tok") % 2
    row = lax.axis_index("tok") // 2
    block = lax.axis_index("ctx")
    where = jnp.stack([row, block]).astype(jnp.int32)
    swap = [(i, i ^ 1) for i in range(tok)]
    forward = [(i, (i + 1) % blocks) for i in range(blocks)]
    backward = [(b, a) for a, b in forward]

    def along(d):
        return [(i, i ^ (2 * d)) for i in range(tok)]

    def across(d):
        return [(c * tok + a, (c + 1) % blocks * tok + b) for c in range(blocks) for a, b in along(d)]

    def both(array, tick):
        local = array[tick, 0]
        return (
            lax.dynamic_index_in_dim(local, core, 0, keepdims=False),
            lax.ppermute(lax.dynamic_index_in_dim(local, 1 - core, 0, keepdims=False), "tok", swap),
        )

    def mine(array):
        return lax.dynamic_index_in_dim(array, core, 0, keepdims=False)

    weighted = (rates[..., None] * values.astype(F32)).astype(BF16)
    state = mine(state_in[0])
    tokens = (*both(keys, 0), *both(weighted, 0))

    partial = first_grads(where, state, *tokens)
    later = after((keys[1:], weighted[1:], queries), partial[0])
    parts = [lax.ppermute(partial[d], ("ctx", "tok"), across(d)) for d in reversed(range(count))]
    next_tokens = (*both(later[0], 0), *both(later[1], 0))
    asks = [both(later[2], 0), both(later[2], 1)]
    shard, square = shard_sum(parts)
    older = lax.ppermute(after(state, shard), "ctx", forward)
    gathered = [shard] + [lax.ppermute(shard, "tok", along(d)) for d in range(1, count)]
    total_sq = total_over(total_over(square, "tok", 1), "head", 1)

    newer, partial = next_grads(where, older, gathered, total_sq, factor, mine(fresh), *next_tokens)
    incoming = jnp.where(block == 0, mine(fresh), newer)
    own = lax.ppermute(newer, "ctx", backward)
    parts = [partial[0]] + [lax.ppermute(partial[d], "tok", along(d)) for d in reversed(range(1, count))]
    shard, square = shard_sum(parts)
    gathered = [shard] + [lax.ppermute(shard, "tok", along(d)) for d in range(1, count)]
    total_sq = total_over(total_over(square, "tok", 1), "head", 1)
    early, early_others = apply_old(own, *asks[0])
    early_back = lax.ppermute(early_others, "tok", swap)
    late, late_others = apply_new(where, incoming, gathered, total_sq, factor, *asks[1])
    late_back = lax.ppermute(late_others, "tok", swap)

    def heads(own, other):
        return jnp.where(core == 0, jnp.stack([own, other]), jnp.stack([other, own]))

    return jnp.stack([heads(early, early_back), heads(late, late_back)])[:, None]


def solution(mesh):
    in_specs = (
        P(None, "ctx", "head", "tok", None),
        P(None, "ctx", "head", "tok", None),
        P(None, "ctx", "head", "tok", None),
        P(None, "ctx", "head", "tok"),
        P("ctx", "head", None, None, None),
        P("head", None, None, None),
    )
    out_specs = P(None, "ctx", "head", "tok", None)
    return jax.shard_map(shards, mesh=mesh, in_specs=in_specs, out_specs=out_specs, check_vma=False)
```
